32 devices in a mesh: ctx: 16 (over z, y, core), fsdp: 2 (over x).
Axes of the slice: x: 2, y: 2, z: 4, core: 2. Of those that a mesh axis runs over, the one named last changes fastest.
Arguments:
- hidden: bfloat16 [2, 2048, 896], P('fsdp', 'ctx'), may hold values from -8 to 8
- pair_of: int32 [16], replicated, may hold values from 0 to 15, each once
- attn_gain: bfloat16 [896], P('fsdp'), may hold values from 0.5 to 1.5
- query_weight: bfloat16 [896, 896], P('fsdp'), may hold values from -1 to 1
- query_bias: bfloat16 [896], P('fsdp'), may hold values from -3 to 3
- key_weight: bfloat16 [896, 128], P('fsdp'), may hold values from -1 to 1
- key_bias: bfloat16 [128], P('fsdp'), may hold values from -3 to 3
- value_weight: bfloat16 [896, 128], P('fsdp'), may hold values from -0.1875 to 0.1875
- value_bias: bfloat16 [128], P('fsdp'), may hold values from -0.59765625 to 0.59765625
- out_weight: bfloat16 [896, 896], P('fsdp'), may hold values from -1 to 1
- mlp_gain: bfloat16 [896], P('fsdp'), may hold values from 0.5 to 1.5
- gate_weight: bfloat16 [896, 4864], P('fsdp'), may hold values from -0.1875 to 0.1875
- up_weight: bfloat16 [896, 4864], P('fsdp'), may hold values from -0.1875 to 0.1875
- down_weight: bfloat16 [4864, 896], P('fsdp'), may hold values from -0.078125 to 0.078125
- cotangent: bfloat16 [2, 2048, 896], P('fsdp', 'ctx'), may hold values from -6 to 6
Outputs:
- output: bfloat16 [2, 2048, 896], P('fsdp', 'ctx')
- input_grad: bfloat16 [2, 2048, 896], P('fsdp', 'ctx')
- attn_gain_grad: float32 [896], P('fsdp')
- query_weight_grad: float32 [896, 896], P('fsdp')
- query_bias_grad: float32 [896], P('fsdp')
- key_weight_grad: float32 [896, 128], P('fsdp')
- key_bias_grad: float32 [128], P('fsdp')
- value_weight_grad: float32 [896, 128], P('fsdp')
- value_bias_grad: float32 [128], P('fsdp')
- out_weight_grad: float32 [896, 896], P('fsdp')
- mlp_gain_grad: float32 [896], P('fsdp')
- gate_weight_grad: float32 [896, 4864], P('fsdp')
- up_weight_grad: float32 [896, 4864], P('fsdp')
- down_weight_grad: float32 [4864, 896], P('fsdp')
The draws below stay inside these ranges and needn't reach their ends.
Inputs may be any that keep to these rules, and one draw needn't show every extreme that they name: A permutation: index c of ctx holds sequence blocks pair_of[c] and 31 - pair_of[c], each of 64 tokens.
All inputs are finite; a program needn't handle non-finite values.
Results may differ from the reference program's by a relative error of at most 0.034.
Values may be sent and summed in bfloat16 or wider, within the bound.
No kernel may reach another device: no remote copies, remote signals or barrier semaphores. Data moves between devices by JAX's collectives and lax.ppermute only.
A program may use at most 320 MiB of HBM per device.

```python
import math
import jax
import jax.numpy as jnp
from jax import lax

D = 896
H = 14
KVH = 2
HD = 64
FF = 4864
TOK_SEQ = 128
LEN = 2048
SEQS = 2
N_CTX = 16


def draw_hidden(key, part):
    baseline = jax.random.normal(jax.random.fold_in(key, 11), (SEQS, LEN, D), jnp.float32)
    values = baseline
    return jnp.clip(values, -8.0, 8.0).astype(jnp.bfloat16)


def draw_query_weight(key, part):
    baseline = jax.random.truncated_normal(jax.random.fold_in(key, 31), -3.0, 3.0, (D, H * HD), jnp.float32) * D ** (-0.5)
    return jnp.clip(baseline, -1.0, 1.0).astype(jnp.bfloat16)


def draw_key_weight(key, part):
    baseline = jax.random.truncated_normal(jax.random.fold_in(key, 41), -3.0, 3.0, (D, KVH * HD), jnp.float32) * D ** (-0.5)
    return jnp.clip(baseline, -1.0, 1.0).astype(jnp.bfloat16)


def level_of(key, dims, cuts, least, top_value):
    level = 1.0
    for position, parts in cuts:
        steps = jax.random.uniform(jax.random.fold_in(jax.random.fold_in(key, 6), position), (parts,), jnp.float32, least / len(cuts), top_value / len(cuts))
        level = level * jnp.repeat(jnp.exp(steps), dims[position] // parts).reshape((-1,) + (1,) * (len(dims) - 1 - position))
    return level


def bell_draw(rng, extent, width, most, cuts=(), kind=jnp.bfloat16):
    values = width * jax.random.normal(rng, extent, jnp.float32)
    if cuts:
        values = values * level_of(rng, extent, cuts, -0.22, 0.18)
    return jnp.clip(values, -most, most).astype(kind)


def setup_inputs(seed: int = 0) -> dict:
    key_list = jax.random.split(jax.random.key(seed), 16)
    return {
        "hidden": draw_hidden(jax.random.fold_in(key_list[15], 71), 0),
        "pair_of": jax.random.permutation(key_list[1], N_CTX).astype(jnp.int32),
        "attn_gain": jnp.clip(1.0 + 0.1 * jax.random.normal(key_list[2], (D,), jnp.float32), 0.5, 1.5).astype(jnp.bfloat16),
        "query_weight": draw_query_weight(jax.random.fold_in(key_list[15], 71), 0),
        "query_bias": bell_draw(key_list[4], (H * HD,), 0.5, 3.0, ((0, 2),)),
        "key_weight": draw_key_weight(jax.random.fold_in(key_list[15], 71), 0),
        "key_bias": bell_draw(key_list[6], (KVH * HD,), 0.5, 3.0, ((0, 2),)),
        "value_weight": bell_draw(key_list[7], (D, KVH * HD), D ** -0.5, 0.1875, ((0, 2),)),
        "value_bias": bell_draw(key_list[8], (KVH * HD,), 0.1, 0.59765625, ((0, 2),)),
        "out_weight": bell_draw(key_list[9], (H * HD, D), (H * HD // 32) ** -0.5, 1.0, ((0, 2),)),
        "mlp_gain": jnp.clip(1.0 + 0.1 * jax.random.normal(key_list[10], (D,), jnp.float32), 0.5, 1.5).astype(jnp.bfloat16),
        "gate_weight": bell_draw(key_list[11], (D, FF), D ** -0.5, 0.1875, ((0, 2),)),
        "up_weight": bell_draw(key_list[12], (D, FF), D ** -0.5, 0.1875, ((0, 2),)),
        "down_weight": bell_draw(key_list[13], (FF, D), FF ** -0.5, 0.078125, ((0, 2),)),
        "cotangent": bell_draw(key_list[14], (SEQS, LEN, D), 1.0, 6.0, ((0, 2), (1, 16))),
    }


@jax.custom_vjp
def low(v):
    return lax.optimization_barrier(v.astype(jnp.bfloat16)).astype(jnp.float32)

@jax.custom_vjp
def low_back(v):
    return v

def low_keep(v):
    return (low(v), None)

def low_pass(kept, grad):
    return (grad,)

def back_keep(v):
    return (v, None)

def back_low(kept, grad):
    return (low(grad),)
low.defvjp(low_keep, low_pass)
low_back.defvjp(back_keep, back_low)
EPSILON = 1e-06
THETA_BASE = 1000000.0

def rotate_half(values):
    middle = values.shape[-1] // 2
    return jnp.concatenate([-values[..., middle:], values[..., :middle]], -1)

def rotary(values, cosine, sine):
    return values * cosine + rotate_half(values) * sine

def normalize(values, gain):
    return values * lax.rsqrt(lax.optimization_barrier(jnp.mean(values * values, -1, keepdims=True)) + EPSILON) * gain

def product(left, right):
    return jnp.dot(left, right, precision=lax.Precision.HIGHEST)

def token_positions(pair_of):
    half_rows = TOK_SEQ // 2
    stored = jnp.arange(LEN, dtype=jnp.int32)
    holder = stored // TOK_SEQ
    second = stored % TOK_SEQ // half_rows
    chosen = jnp.take(pair_of, holder)
    block = jnp.where(second == 0, chosen, 2 * N_CTX - 1 - chosen)
    return (block * half_rows + stored % half_rows).astype(jnp.int32)

def rotary_tables(positions):
    middle = HD // 2
    freqs = jnp.power(THETA_BASE, -2.0 * jnp.arange(middle, dtype=jnp.float32) / HD)
    angle = positions.astype(jnp.float32)[:, None] * freqs[None, :]
    angle = jnp.concatenate([angle, angle], -1)[:, None, :]
    return (jnp.cos(angle), jnp.sin(angle))

def one_sequence(params, inputs, positions, cosine, sine):
    attn_gain, query_weight, query_bias, key_weight, key_bias, value_weight, value_bias, out_weight, mlp_gain, gate_weight, up_weight, down_weight = params
    groups = H // KVH
    score_scale = 1.0 / math.sqrt(HD)
    normed_one = low(normalize(inputs, attn_gain))
    queries = low_back(product(normed_one, query_weight) + query_bias).reshape(LEN, H, HD)
    keys = low_back(product(normed_one, key_weight) + key_bias).reshape(LEN, KVH, HD)
    values = low(low_back(product(normed_one, value_weight) + value_bias)).reshape(LEN, KVH, HD)
    queries = low(rotary(queries, cosine, sine)).reshape(LEN, KVH, groups, HD)
    keys = low(rotary(keys, cosine, sine))
    query_block = math.gcd(256, LEN)

    def attend_block(pieces):
        block_queries, block_positions = pieces
        scores = jnp.einsum('qkgd,tkd->kgqt', block_queries, keys, precision=lax.Precision.HIGHEST) * score_scale
        scores = low_back(scores)
        allowed = positions[None, :] <= block_positions[:, None]
        probs = low(jax.nn.softmax(jnp.where(allowed, scores, -jnp.inf), axis=-1))
        mixed = jnp.einsum('kgqt,tkd->qkgd', probs, values, precision=lax.Precision.HIGHEST)
        return mixed.reshape(block_queries.shape[0], H * HD)
    blocks = LEN // query_block
    heads = lax.map(jax.checkpoint(attend_block), (queries.reshape(blocks, query_block, KVH, groups, HD), positions.reshape(blocks, query_block)))
    heads = low(low_back(heads.reshape(LEN, H * HD)))
    resid = inputs + low_back(product(heads, out_weight))
    normed_two = low(normalize(resid, mlp_gain))
    gate_values = low_back(product(normed_two, gate_weight))
    up_values = low_back(product(normed_two, up_weight))
    activation = low(jax.nn.silu(gate_values) * up_values)
    return resid + low_back(product(activation, down_weight))

def reference(hidden, pair_of, attn_gain, query_weight, query_bias, key_weight, key_bias, value_weight, value_bias, out_weight, mlp_gain, gate_weight, up_weight, down_weight, cotangent):
    positions = token_positions(pair_of)
    cosine, sine = rotary_tables(positions)
    params = tuple((weight.astype(jnp.float32) for weight in (attn_gain, query_weight, query_bias, key_weight, key_bias, value_weight, value_bias, out_weight, mlp_gain, gate_weight, up_weight, down_weight)))
    inputs = hidden.astype(jnp.float32)

    def forward(weights, activations):
        return lax.map(lambda single: one_sequence(weights, single, positions, cosine, sine), activations)
    result, pullback = jax.vjp(forward, params, inputs)
    grads, input_grad = pullback(cotangent.astype(jnp.float32))
    return (result.astype(jnp.bfloat16), input_grad.astype(jnp.bfloat16), grads[0], grads[1], grads[2], grads[3], grads[4], grads[5], grads[6], grads[7], grads[8], grads[9], grads[10], grads[11])
```

```python
import math

import jax
import jax.numpy as jnp
from jax import lax
from jax.sharding import PartitionSpec as P

H = 14
KVH = 2
HD = 64

EPSILON = 1e-06
THETA_BASE = 1000000.0

BF16 = jnp.bfloat16
F32 = jnp.float32


def rotate_half(values):
    middle = values.shape[-1] // 2
    return jnp.concatenate([-values[..., middle:], values[..., :middle]], -1)


def rotate_back(values):
    middle = values.shape[-1] // 2
    return jnp.concatenate([values[..., middle:], -values[..., :middle]], -1)


def rotary(values, cosine, sine):
    return values * cosine + rotate_half(values) * sine


def rotary_back(values, cosine, sine):
    return values * cosine + rotate_back(values * sine)


def rotary_tables(positions):
    middle = HD // 2
    freqs = jnp.power(THETA_BASE, -2.0 * jnp.arange(middle, dtype=F32) / HD)
    angle = positions.astype(F32)[:, None] * freqs[None, :]
    angle = jnp.concatenate([angle, angle], -1)[:, None, :]
    return (jnp.cos(angle), jnp.sin(angle))


def normalize(values, gain):
    inverse = lax.rsqrt(jnp.mean(values * values, -1, keepdims=True) + EPSILON)
    return (values * inverse * gain, inverse)


def norm_back(values, inverse, gain, grad):
    scaled = gain * grad
    mean_term = jnp.mean(scaled * values, -1, keepdims=True)
    return inverse * scaled - values * inverse**3 * mean_term


def dot(left, right, left_dim=1, right_dim=0):
    return lax.dot_general(
        left, right, (((left_dim,), (right_dim,)), ((), ())), preferred_element_type=F32
    )


class Ring:
    def __init__(self, n_ctx):
        self.chips = n_ctx // 2
        evens = list(range(0, self.chips, 2))
        odds = list(range(1, self.chips, 2))
        self.order = evens + odds[::-1]
        count = self.chips
        self.up = [
            (2 * self.order[i] + core, 2 * self.order[(i + 1) % count] + core)
            for i in range(count)
            for core in range(2)
        ]
        self.down = [(b, a) for a, b in self.up]
        self.swap = [(i, i ^ 1) for i in range(n_ctx)]
        me = lax.axis_index("ctx")
        self.core = me % 2
        chip = me // 2
        self.place = jnp.where(chip % 2 == 0, chip // 2, count - 1 - chip // 2)
        self.offsets = [0]
        for step in range(1, count // 2):
            self.offsets += [-step, step]
        self.offsets.append(count // 2)
        places = (self.place + jnp.array(self.offsets, jnp.int32)) % count
        chips = jnp.where(places < (count + 1) // 2, 2 * places, 2 * (count - 1 - places) + 1)
        self.places = places
        self.own_devices = 2 * chips + self.core
        self.other_devices = 2 * chips + 1 - self.core

    def send_up(self, block):
        return lax.ppermute(block, "ctx", self.up)

    def send_down(self, block):
        return lax.ppermute(block, "ctx", self.down)

    def swap_core(self, block):
        return lax.ppermute(block, "ctx", self.swap)

    def gather(self, block):
        half = block.shape[0] // 2
        steps = self.chips // 2
        blocks = [block]
        low = high = block
        for _ in range(steps - 1):
            low = self.send_up(low)
            high = self.send_down(high)
            blocks += [low, high]
        far = jnp.concatenate([self.send_up(low[:half]), self.send_down(high[half:])], 0)
        return blocks + [far]

    def gather_all(self, block):
        own = self.gather(block)
        other = [self.swap_core(part) for part in own]
        return own + other

    def add(self, left, right):
        return (left.astype(F32) + right.astype(F32)).astype(BF16)

    def scatter(self, blocks):
        steps = self.chips // 2
        half = blocks[0].shape[0] // 2
        at = dict(zip(self.offsets, blocks))
        far = at[steps]
        low = self.send_up(far[:half])
        high = self.send_down(far[half:])
        for step in range(steps - 1, 0, -1):
            ahead, behind = at[step], at[-step]
            if step == steps - 1:
                ahead = jnp.concatenate([self.add(ahead[:half], low), ahead[half:]], 0)
                behind = jnp.concatenate([behind[:half], self.add(behind[half:], high)], 0)
            else:
                ahead = self.add(ahead, low)
                behind = self.add(behind, high)
            low = self.send_up(ahead)
            high = self.send_down(behind)
        return at[0].astype(F32) + low.astype(F32) + high.astype(F32)

    def scatter_all(self, partial):
        count = self.chips
        received = self.swap_core(partial[count:])
        mine = self.add(partial[:count], received)
        return self.scatter([mine[i] for i in range(count)])


def attend(query_group, first_position, keyval_order, tile_rows, key_width, score_scale):
    seq_count, block_rows, kv_heads, groups, head_size = query_group.shape
    query_pos = first_position + jnp.arange(block_rows, dtype=jnp.int32)
    tile_count = (first_position + block_rows + tile_rows - 1) // tile_rows

    def tile_step(tile_index, carried):
        running_max, running_sum, weighted = carried
        piece = lax.dynamic_slice_in_dim(keyval_order, tile_index * tile_rows, tile_rows, 1)
        keys = piece[..., :key_width].reshape(seq_count, tile_rows, kv_heads, head_size)
        values = piece[..., key_width:].reshape(seq_count, tile_rows, kv_heads, head_size)
        scores = (
            jnp.einsum("sqkgd,stkd->skgqt", query_group, keys, preferred_element_type=F32)
            * score_scale
        )
        key_pos = tile_index * tile_rows + jnp.arange(tile_rows, dtype=jnp.int32)
        allowed = key_pos[None, :] <= query_pos[:, None]
        scores = jnp.where(allowed, scores, -jnp.inf)
        fresh_max = jnp.maximum(running_max, jnp.max(scores, -1))
        weights = jnp.exp(scores - fresh_max[..., None])
        factor = jnp.exp(running_max - fresh_max)
        running_sum = running_sum * factor + jnp.sum(weights, -1)
        update = jnp.einsum(
            "skgqt,stkd->skgqd", weights.astype(BF16), values, preferred_element_type=F32
        )
        weighted = weighted * factor[..., None] + update
        return (fresh_max, running_sum, weighted)

    start_state = (
        jnp.full((seq_count, kv_heads, groups, block_rows), -jnp.inf, F32),
        jnp.zeros((seq_count, kv_heads, groups, block_rows), F32),
        jnp.zeros((seq_count, kv_heads, groups, block_rows, head_size), F32),
    )
    running_max, running_sum, weighted = lax.fori_loop(0, tile_count, tile_step, start_state)
    return (weighted / running_sum[..., None], running_max + jnp.log(running_sum))


def attend_back(
    query_group,
    first_position,
    keyval_order,
    grad_group,
    delta,
    log_total,
    grad_keyval,
    tile_rows,
    key_width,
    score_scale,
):
    seq_count, block_rows, kv_heads, groups, head_size = query_group.shape
    query_pos = first_position + jnp.arange(block_rows, dtype=jnp.int32)
    tile_count = (first_position + block_rows + tile_rows - 1) // tile_rows

    def tile_step(tile_index, carried):
        grad_query, grad_pairs = carried
        piece = lax.dynamic_slice_in_dim(keyval_order, tile_index * tile_rows, tile_rows, 1)
        keys = piece[..., :key_width].reshape(seq_count, tile_rows, kv_heads, head_size)
        values = piece[..., key_width:].reshape(seq_count, tile_rows, kv_heads, head_size)
        scores = (
            jnp.einsum("sqkgd,stkd->skgqt", query_group, keys, preferred_element_type=F32)
            * score_scale
        )
        key_pos = tile_index * tile_rows + jnp.arange(tile_rows, dtype=jnp.int32)
        allowed = key_pos[None, :] <= query_pos[:, None]
        probs = jnp.exp(jnp.where(allowed, scores, -jnp.inf) - log_total[..., None])
        grad_values = jnp.einsum(
            "skgqt,sqkgd->stkd", probs.astype(BF16), grad_group, preferred_element_type=F32
        )
        grad_probs = jnp.einsum("sqkgd,stkd->skgqt", grad_group, values, preferred_element_type=F32)
        grad_scores = (probs * (grad_probs - delta[..., None])).astype(BF16)
        grad_query = (
            grad_query
            + jnp.einsum("skgqt,stkd->sqkgd", grad_scores, keys, preferred_element_type=F32)
            * score_scale
        )
        grad_keys = (
            jnp.einsum("skgqt,sqkgd->stkd", grad_scores, query_group, preferred_element_type=F32)
            * score_scale
        )
        joined = jnp.concatenate(
            [
                grad_keys.reshape(seq_count, tile_rows, key_width),
                grad_values.reshape(seq_count, tile_rows, key_width),
            ],
            -1,
        )
        previous = lax.dynamic_slice_in_dim(grad_pairs, tile_index * tile_rows, tile_rows, 1)
        grad_pairs = lax.dynamic_update_slice_in_dim(
            grad_pairs, previous + joined, tile_index * tile_rows, 1
        )
        return (grad_query, grad_pairs)

    start_state = (
        jnp.zeros((seq_count, block_rows, kv_heads, groups, head_size), F32),
        grad_keyval,
    )
    return lax.fori_loop(0, tile_count, tile_step, start_state)


def on_device(
    hidden,
    pair_of,
    attn_gain,
    query_weight,
    query_bias,
    key_weight,
    key_bias,
    value_weight,
    value_bias,
    out_weight,
    mlp_gain,
    gate_weight,
    up_weight,
    down_weight,
    cotangent,
):
    n_ctx = lax.axis_size("ctx")
    ring = Ring(n_ctx)
    chips = n_ctx // 2
    place = lax.axis_index("ctx")
    side = lax.axis_index("fsdp")
    core = ring.core
    flip = [(0, 1), (1, 0)]

    def swap_side(value):
        return lax.ppermute(value, "fsdp", flip)

    def by_side(own, other, axis=0):
        return jnp.where(
            side == 0,
            jnp.concatenate([own, other], axis),
            jnp.concatenate([other, own], axis),
        )

    local_rows, model_width = hidden.shape[1:]
    half_rows = local_rows // 2
    half_width = model_width // 2
    key_width = key_weight.shape[1]
    groups = H // KVH
    score_scale = 1.0 / math.sqrt(HD)
    ffn_half = down_weight.shape[0] // n_ctx
    ffn_cols = 2 * ffn_half

    hidden_own = hidden[0]
    grad_own = cotangent[0]

    small_sizes = (half_width, half_width, half_width, key_width // 2, key_width // 2)
    small_own = jnp.concatenate([attn_gain, mlp_gain, query_bias, key_bias, value_bias])
    small_other = swap_side(small_own)
    smalls = []
    start = 0
    for size in small_sizes:
        smalls.append(by_side(small_own[start : start + size], small_other[start : start + size]))
        start += size
    gain_one, gain_two, qbias, kbias, vbias = [value.astype(F32) for value in smalls]

    attn_own = jnp.concatenate([query_weight, key_weight, value_weight, out_weight], 1)
    quarter = half_width // 2
    attn_piece = swap_side(lax.dynamic_slice_in_dim(attn_own, core * quarter, quarter, 0))
    attn_rest = ring.swap_core(attn_piece)
    attn_other = jnp.where(
        core == 0,
        jnp.concatenate([attn_piece, attn_rest], 0),
        jnp.concatenate([attn_rest, attn_piece], 0),
    )
    attn_full = by_side(attn_own, attn_other)
    query_full = attn_full[:, :model_width]
    keyval_full = attn_full[:, model_width : model_width + 2 * key_width]
    out_full = attn_full[:, model_width + 2 * key_width :]

    hidden_parts = ring.gather_all(hidden_own)
    hidden_all = jnp.concatenate(hidden_parts, 0)

    def ffn_slice(weight):
        return jnp.concatenate(
            [
                lax.dynamic_slice_in_dim(weight, place * ffn_half, ffn_half, 1),
                lax.dynamic_slice_in_dim(
                    weight, weight.shape[1] // 2 + place * ffn_half, ffn_half, 1
                ),
            ],
            1,
        )

    gate_own = ffn_slice(gate_weight)
    up_own = ffn_slice(up_weight)
    down_own = lax.dynamic_slice_in_dim(down_weight, place * ffn_half, ffn_half, 0)
    gate_mine = by_side(gate_own, swap_side(gate_own))
    up_mine = by_side(up_own, swap_side(up_own))
    down_mine = by_side(down_own, swap_side(down_own))

    devices = jnp.concatenate([ring.own_devices, ring.other_devices])
    pairs = jnp.sum(
        jnp.where(devices[:, None] == jnp.arange(n_ctx, dtype=jnp.int32)[None], pair_of[None], 0),
        1,
    )
    blocks_of = jnp.stack([pairs, 2 * n_ctx - 1 - pairs], 1).reshape(-1)
    listed = jnp.arange(2 * n_ctx, dtype=jnp.int32)
    place_of = jnp.sum(jnp.where(blocks_of[None, :] == listed[:, None], listed[None, :], 0), 1)
    offsets = jnp.arange(half_rows, dtype=jnp.int32)
    positions = (blocks_of[:, None] * half_rows + offsets[None, :]).reshape(-1)
    cosine, sine = rotary_tables(positions)
    cosine_own, sine_own = cosine[:local_rows], sine[:local_rows]
    starts = [blocks_of[0] * half_rows, blocks_of[1] * half_rows]

    normed_all, _ = normalize(hidden_all.astype(F32), gain_one)
    normed_all = normed_all.astype(BF16)
    inputs = hidden_own.astype(F32)
    normed_one, inverse_one = normalize(inputs, gain_one)
    normed_one = normed_one.astype(BF16)
    total_rows = hidden_all.shape[0]

    keyval = dot(normed_all, keyval_full) + jnp.concatenate([kbias, vbias])
    keys = rotary(keyval[:, :key_width].reshape(total_rows, KVH, HD), cosine, sine)
    keyval_rel = jnp.concatenate(
        [keys.reshape(total_rows, key_width).astype(BF16), keyval[:, key_width:].astype(BF16)], 1
    )
    keyval_order = jnp.take(
        keyval_rel.reshape(2 * n_ctx, half_rows, 2 * key_width), place_of, axis=0
    ).reshape(1, total_rows, 2 * key_width)
    queries = rotary(
        (dot(normed_one, query_full) + qbias).reshape(local_rows, H, HD), cosine_own, sine_own
    ).astype(BF16)

    tile_rows = math.gcd(1024, total_rows)
    query_groups = queries.reshape(1, local_rows, KVH, groups, HD)
    head_outs = []
    log_totals = []
    for slot in range(2):
        head_out, log_total = attend(
            query_groups[:, slot * half_rows : (slot + 1) * half_rows],
            starts[slot],
            keyval_order,
            tile_rows,
            key_width,
            score_scale,
        )
        head_outs.append(head_out)
        log_totals.append(log_total)
    heads = jnp.concatenate(
        [part.transpose(0, 3, 1, 2, 4).reshape(half_rows, H * HD) for part in head_outs], 0
    ).astype(BF16)
    resid = inputs + dot(heads, out_full)
    normed_two, inverse_two = normalize(resid, gain_two)
    normed_two = normed_two.astype(BF16)

    grad_all = jnp.concatenate(ring.gather_all(grad_own), 0)
    two_all = jnp.concatenate(ring.gather_all(normed_two), 0)
    gate_values = dot(two_all, gate_mine)
    up_values = dot(two_all, up_mine)
    sigmoid_gate = jax.nn.sigmoid(gate_values)
    silu_gate = gate_values * sigmoid_gate
    activation = (silu_gate * up_values).astype(BF16)
    grad_act = dot(grad_all, down_mine, 1, 1)
    grad_gate = (
        grad_act * up_values * sigmoid_gate * (1.0 + gate_values * (1.0 - sigmoid_gate))
    ).astype(BF16)
    grad_up = (grad_act * silu_gate).astype(BF16)
    grad_two_part = (dot(grad_gate, gate_mine, 1, 1) + dot(grad_up, up_mine, 1, 1)).astype(BF16)
    grad_two = ring.scatter_all(grad_two_part.reshape(n_ctx, local_rows, model_width))
    output_part = dot(activation, down_mine).astype(BF16)
    output = (
        resid + ring.scatter_all(output_part.reshape(n_ctx, local_rows, model_width))
    ).astype(BF16)

    down_part = dot(activation, grad_all, 0, 0).astype(BF16).reshape(2, ffn_half, model_width)

    def keep_send(first, second):
        return jnp.where(side == 0, first, second), jnp.where(side == 0, second, first)

    def fold(first, second):
        keep, send = keep_send(first, second)
        return (keep.astype(F32) + swap_side(send).astype(F32)).astype(BF16)

    def hidden_unit_grad(grad):
        full = dot(grad, two_all, 0, 0).astype(BF16)
        total = fold(full[:, :half_width], full[:, half_width:])
        return jnp.concatenate([total[:ffn_half], total[ffn_half:]], 1)

    down_total = fold(down_part[0], down_part[1])
    gate_total = hidden_unit_grad(grad_gate)
    up_total = hidden_unit_grad(grad_up)
    ffn_grads = lax.all_gather(
        jnp.stack([down_total, gate_total, up_total]), "ctx", axis=1, tiled=True
    )
    down_grad = ffn_grads[0].astype(F32)

    def unit_rows(gathered):
        return jnp.concatenate(
            [gathered[:, :half_width].T, gathered[:, half_width:].T], 1
        ).astype(F32)

    gate_grad = unit_rows(ffn_grads[1])
    up_grad = unit_rows(ffn_grads[2])

    gain_two_part = jnp.sum(grad_two * resid * inverse_two, 0)
    grad_resid = grad_own.astype(F32) + norm_back(resid, inverse_two, gain_two, grad_two)
    grad_attn = grad_resid.astype(BF16)
    out_part = dot(heads, grad_attn, 0, 0)
    grad_heads = dot(grad_attn, out_full, 1, 1).astype(BF16)
    grad_groups = grad_heads.reshape(1, local_rows, KVH, groups, HD)
    grad_keyval = jnp.zeros((1, total_rows, 2 * key_width), F32)
    grad_query_parts = []
    for slot in range(2):
        grad_slot = grad_groups[:, slot * half_rows : (slot + 1) * half_rows]
        delta = jnp.einsum("sqkgd,skgqd->skgq", grad_slot.astype(F32), head_outs[slot])
        grad_query, grad_keyval = attend_back(
            query_groups[:, slot * half_rows : (slot + 1) * half_rows],
            starts[slot],
            keyval_order,
            grad_slot,
            delta,
            log_totals[slot],
            grad_keyval,
            tile_rows,
            key_width,
            score_scale,
        )
        grad_query_parts.append(grad_query)
    grad_query_rot = jnp.concatenate(grad_query_parts, 1).reshape(local_rows, H, HD)
    grad_query_pre = rotary_back(grad_query_rot, cosine_own, sine_own).reshape(
        local_rows, H * HD
    )
    grad_keyval_rel = jnp.take(
        grad_keyval.reshape(2 * n_ctx, half_rows, 2 * key_width), blocks_of, axis=0
    ).reshape(total_rows, 2 * key_width)
    grad_key_pre = rotary_back(
        grad_keyval_rel[:, :key_width].reshape(total_rows, KVH, HD), cosine, sine
    ).reshape(total_rows, key_width)
    keyval_part32 = jnp.concatenate([grad_key_pre, grad_keyval_rel[:, key_width:]], 1)
    keyval_part = keyval_part32.astype(BF16)
    grad_keyval_own = ring.scatter_all(
        keyval_part.reshape(n_ctx, local_rows, 2 * key_width)
    ).astype(BF16)
    qbias_part = jnp.sum(grad_query_pre, 0)
    kvbias_part = jnp.sum(keyval_part32, 0)
    grad_query_pre = grad_query_pre.astype(BF16)
    query_part = dot(normed_one, grad_query_pre, 0, 0)
    keyval_grad_part = dot(normed_all, keyval_part, 0, 0)
    gain_one_part = (
        jnp.sum(query_part * query_full.astype(F32), 1)
        + jnp.sum(keyval_grad_part * keyval_full.astype(F32), 1)
    ) / gain_one

    grad_one = dot(grad_query_pre, query_full, 1, 1) + dot(grad_keyval_own, keyval_full, 1, 1)
    input_grad = (grad_resid + norm_back(inputs, inverse_one, gain_one, grad_one)).astype(BF16)

    pad_rows = 16
    wide = jnp.concatenate([query_part, keyval_grad_part, out_part], 1).astype(BF16)
    wide_cols = wide.shape[1]
    small_rows = []
    for index in range(2):
        pieces = [
            gain_one_part[index * half_width : (index + 1) * half_width],
            gain_two_part[index * half_width : (index + 1) * half_width],
            qbias_part[index * half_width : (index + 1) * half_width],
            kvbias_part[index * key_width // 2 : (index + 1) * key_width // 2],
            kvbias_part[key_width + index * key_width // 2 : key_width + (index + 1) * key_width // 2],
        ]
        row = jnp.concatenate(pieces)
        row = jnp.pad(row, (0, wide_cols - row.shape[0])).astype(BF16)
        small_rows.append(jnp.pad(row[None], ((0, pad_rows - 1), (0, 0))))
    packed = jnp.stack(
        [
            jnp.concatenate([wide[:half_width], small_rows[0]], 0),
            jnp.concatenate([wide[half_width:], small_rows[1]], 0),
        ]
    )
    half_cols = wide_cols // 2
    left, right = packed[:, :, :half_cols], packed[:, :, half_cols:]
    keep = jnp.where(core == 0, left, right)
    send = jnp.where(core == 0, right, left)
    chip_part = ring.add(keep, ring.swap_core(send))
    side_part = fold(chip_part[0], chip_part[1])
    pack_rows = side_part.shape[0]
    cut = half_cols // chips
    cuts = side_part.reshape(pack_rows, chips, cut).transpose(1, 0, 2)
    listed_cuts = jnp.take(cuts, ring.places, axis=0)
    total = ring.scatter([listed_cuts[i] for i in range(chips)]).astype(BF16)
    back = jnp.zeros((chips, pack_rows, cut), BF16)
    for index, part in enumerate(ring.gather(total)):
        back = lax.dynamic_update_index_in_dim(back, part, ring.places[index], 0)
    mine = back.transpose(1, 0, 2).reshape(pack_rows, half_cols)
    theirs = ring.swap_core(mine)
    whole = jnp.where(
        core == 0, jnp.concatenate([mine, theirs], 1), jnp.concatenate([theirs, mine], 1)
    ).astype(F32)
    wide_total = whole[:half_width]
    row = whole[half_width]
    bounds = []
    start = 0
    for size in small_sizes:
        bounds.append(row[start : start + size])
        start += size
    gain_one_total, gain_two_total, qbias_total, kbias_total, vbias_total = bounds
    cols = (
        model_width,
        model_width + key_width,
        model_width + 2 * key_width,
    )
    return (
        output[None],
        input_grad[None],
        gain_one_total,
        wide_total[:, : cols[0]],
        qbias_total,
        wide_total[:, cols[0] : cols[1]],
        kbias_total,
        wide_total[:, cols[1] : cols[2]],
        vbias_total,
        wide_total[:, cols[2] :],
        gain_two_total,
        gate_grad,
        up_grad,
        down_grad,
    )


def solution(mesh):
    in_specs = (
        P("fsdp", "ctx", None),
        P(),
        P("fsdp"),
        P("fsdp", None),
        P("fsdp"),
        P("fsdp", None),
        P("fsdp"),
        P("fsdp", None),
        P("fsdp"),
        P("fsdp", None),
        P("fsdp"),
        P("fsdp", None),
        P("fsdp", None),
        P("fsdp", None),
        P("fsdp", "ctx", None),
    )
    out_specs = (
        P("fsdp", "ctx", None),
        P("fsdp", "ctx", None),
        P("fsdp"),
        P("fsdp", None),
        P("fsdp"),
        P("fsdp", None),
        P("fsdp"),
        P("fsdp", None),
        P("fsdp"),
        P("fsdp", None),
        P("fsdp"),
        P("fsdp", None),
        P("fsdp", None),
        P("fsdp", None),
    )
    return jax.shard_map(
        on_device, mesh=mesh, in_specs=in_specs, out_specs=out_specs, check_vma=False
    )
```
